32 devices in a mesh: section: 16 (over z, y, core), dp: 2 (over x).
Axes of the slice: x: 2, y: 2, z: 4, core: 2. Of those that a mesh axis runs over, the one named last changes fastest.
Arguments:
- section_states: bfloat16 [16, 4, 2, 16, 16, 512], P('section', None, 'dp'), may hold values from -6 to 6
- conv_kernels: bfloat16 [16, 2, 1152, 512], P('section'), may hold values from -0.1875 to 0.1875
- top_feed: bfloat16 [3, 4, 2, 16, 16, 512], P(None, None, 'dp'), may hold values from -6 to 6
Outputs:
- final_states: bfloat16 [16, 4, 2, 16, 16, 512], P('section', None, 'dp')
- kernel_grads: float32 [16, 2, 1152, 512], P('section', None, 'dp')
The draws below stay inside these ranges and needn't reach their ends.
All inputs are finite; a program needn't handle non-finite values.
Results may differ from the reference program's by a relative error of at most 0.024.
Values may be sent and summed in bfloat16 or wider, within the bound.
A program may use at most 128 MiB of HBM per device.

```python
import jax
import jax.numpy as jnp
from jax import lax

CH = 512
GW = 128
HW = 16
TICKS = 4
IMAGES = 2
SECTIONS = 16


def steps_of(rng, extent, split, least, largest):
    def one(axis_at, shards_of):
        heights = jax.random.uniform(jax.random.fold_in(jax.random.fold_in(rng, 6), axis_at), (shards_of,), jnp.float32, least / len(split), largest / len(split))
        return jnp.repeat(jnp.exp(heights), extent[axis_at] // shards_of).reshape((-1,) + (1,) * (len(extent) - axis_at - 1))

    level = one(*split[0])
    for cut in split[1:]:
        level = level * one(*cut)
    return level


def bell_draw(own_key, dims, deviation, bound, cuts=(), held_as=jnp.bfloat16):
    factor_of = steps_of(own_key, dims, cuts, -0.22, 0.18) if cuts else 1.0
    entries = jax.random.normal(own_key, dims, jnp.float32) * deviation * factor_of
    return jnp.minimum(jnp.maximum(entries, -bound), bound).astype(held_as)


def setup_inputs(seed: int = 0) -> dict:
    keys = jax.random.split(jax.random.key(seed), 4)
    return {
        "section_states": bell_draw(keys[0], (SECTIONS, 4, IMAGES, HW, HW, CH), 1.0, 6.0, ((0, 16), (2, 2))),
        "conv_kernels": bell_draw(keys[1], (SECTIONS, 2, 9 * GW, CH), (9 * GW) ** -0.5, 0.1875, ((0, 16),)),
        "top_feed": bell_draw(keys[2], (TICKS - 1, 4, IMAGES, HW, HW, CH), 1.0, 6.0, ((2, 2),)),
    }


def tap_stack(field):
    height = field.shape[1]
    width = field.shape[2]
    padded = jnp.pad(field, ((0, 0), (1, 1), (1, 1), (0, 0)))
    pieces = [padded[:, row_off:row_off + height, col_off:col_off + width, :] for row_off in range(3) for col_off in range(3)]
    stacked = jnp.stack(pieces, axis=3)
    return stacked.reshape(field.shape[0] * height * width, 9, field.shape[3] // GW, GW)

def smooth_grad(value):
    sigma = jax.nn.sigmoid(value)
    return sigma * (1.0 + value * (1.0 - sigma))

def kernel_view(kernel):
    return kernel.reshape(9, GW, kernel.shape[1] // GW, GW).astype(jnp.float32)

def conv_apply(taps, kernel, shape):
    result = jnp.einsum('nkgi,kigo->ngo', taps.astype(jnp.float32), kernel_view(kernel))
    return result.reshape(shape)

def conv_back(grad_field, kernel):
    taps = tap_stack(grad_field)[:, ::-1]
    result = jnp.einsum('nkgo,kigo->ngi', taps.astype(jnp.float32), kernel_view(kernel))
    return result.reshape(grad_field.shape)

def kernel_term(taps, grad_field):
    count = taps.shape[0]
    flat = grad_field.reshape(count, taps.shape[2], GW).astype(jnp.float32)
    result = jnp.einsum('nkgi,ngo->kigo', taps.astype(jnp.float32), flat)
    return result.reshape(9 * GW, taps.shape[2] * GW)

def coupling_back(state, kernels):
    shape = state.shape[1:]
    output_one = state[0].astype(jnp.float32)
    output_two = state[1].astype(jnp.float32)
    grad_one = state[2]
    grad_two = state[3]
    act_one = jax.nn.silu(output_one).astype(jnp.bfloat16)
    taps_one = tap_stack(act_one)
    input_two = (output_two - conv_apply(taps_one, kernels[1], shape)).astype(jnp.bfloat16)
    wide_two = input_two.astype(jnp.float32)
    act_two = jax.nn.silu(wide_two).astype(jnp.bfloat16)
    taps_two = tap_stack(act_two)
    input_one = (output_one - conv_apply(taps_two, kernels[0], shape)).astype(jnp.bfloat16)
    total_one = (grad_one.astype(jnp.float32) + conv_back(grad_two, kernels[1]) * smooth_grad(output_one)).astype(jnp.bfloat16)
    term_second = kernel_term(taps_one, grad_two)
    grad_input_two = (grad_two.astype(jnp.float32) + conv_back(total_one, kernels[0]) * smooth_grad(wide_two)).astype(jnp.bfloat16)
    term_first = kernel_term(taps_two, total_one)
    return (jnp.stack([input_one, input_two, total_one, grad_input_two]), jnp.stack([term_first, term_second]))

def run_section(pair):
    return coupling_back(pair[0], pair[1])

def reference(section_states, conv_kernels, top_feed):
    current = section_states
    total = jnp.zeros(conv_kernels.shape, jnp.float32)
    produced = section_states
    for tick in range(TICKS):
        produced, grads = lax.map(run_section, (current, conv_kernels))
        total = total + grads
        if tick + 1 < TICKS:
            current = jnp.concatenate([produced[1:], top_feed[tick][None]], axis=0)
    return (produced, total * (1.0 / (HW * HW)))
```

```python
import functools

import jax
import jax.numpy as jnp
from jax import lax
from jax.experimental import pallas as pl
from jax.experimental.pallas import tpu as pltpu
from jax.sharding import PartitionSpec as P

GW = 128
WIDTH = 2
MESH = pl.DeviceIdType.MESH


def smooth_grad(value):
    sigma = jax.nn.sigmoid(value)
    return sigma * (1.0 + value * (1.0 - sigma))


def fused_kernel(
    dims,
    states_ref,
    kernels_ref,
    feed_ref,
    final_ref,
    grads_ref,
    inbuf,
    outbuf,
    weights,
    taps,
    acc,
    gsend,
    gown,
    grecv,
    gout,
    in_sem,
    send_sem,
    weight_sem,
    final_sem,
    gsend_sem,
    grecv_sem,
    gout_sem,
):
    ticks, groups, images, height, width, share, shards = dims
    cells = height * width
    rows = images * cells
    pad = (height + 2) * width
    me = lax.axis_index("section")
    count = lax.axis_size("section")
    mine = lax.axis_index("dp")
    is_top = me == count - 1
    has_below = me > 0

    def lanes(group):
        start = group * GW
        return pl.ds(start if isinstance(group, int) else pl.multiple_of(start, GW), GW)

    def first_copy(group, stream):
        return pltpu.make_async_copy(
            states_ref.at[stream, :, lanes(group)],
            inbuf.at[0, group, stream],
            in_sem.at[0, group, stream],
        )

    def feed_copy(tick, group, stream):
        return pltpu.make_async_copy(
            feed_ref.at[tick - 1, stream, :, lanes(group)],
            inbuf.at[tick, group, stream],
            in_sem.at[tick, group, stream],
        )

    def weight_copy(group, branch):
        return pltpu.make_async_copy(
            kernels_ref.at[branch, :, lanes(group)],
            weights.at[branch, group],
            weight_sem.at[branch, group],
        )

    def final_copy(group, stream):
        return pltpu.make_async_copy(
            outbuf.at[ticks - 1, group, stream],
            final_ref.at[stream, :, lanes(group)],
            final_sem.at[group, stream],
        )

    def below_copy(tick, group, stream):
        return pltpu.make_async_remote_copy(
            src_ref=outbuf.at[tick, group, stream],
            dst_ref=inbuf.at[tick + 1, group, stream],
            send_sem=send_sem.at[tick, group, stream],
            recv_sem=in_sem.at[tick + 1, group, stream],
            device_id={"section": me - 1},
            device_id_type=MESH,
        )

    def share_copy(group, branch, offset):
        partner = lax.rem(mine + offset, shards)
        return pltpu.make_async_remote_copy(
            src_ref=gsend.at[branch, group, pl.ds(pl.multiple_of(partner * share, 16), share)],
            dst_ref=grecv.at[offset - 1, branch, group],
            send_sem=gsend_sem.at[offset - 1, branch, group],
            recv_sem=grecv_sem.at[offset - 1, branch, group],
            device_id={"dp": partner},
            device_id_type=MESH,
        )

    def gout_copy(group, branch):
        return pltpu.make_async_copy(
            gout.at[branch, group],
            grads_ref.at[branch, :, lanes(group)],
            gout_sem.at[branch, group],
        )

    for group in range(groups):
        for stream in range(4):
            first_copy(group, stream).start()
        for branch in range(2):
            weight_copy(group, branch).start()

    @pl.when(is_top)
    def _():
        @pl.loop(1, ticks)
        def _(tick):
            for group in range(groups):
                for stream in range(4):
                    feed_copy(tick, group, stream).start()

    barrier = pltpu.get_barrier_semaphore()

    @pl.when(has_below)
    def _():
        pl.semaphore_signal(barrier, inc=1, device_id={"section": me - 1}, device_id_type=MESH)

    @pl.when(jnp.logical_not(is_top))
    def _():
        pl.semaphore_signal(barrier, inc=1, device_id={"section": me + 1}, device_id_type=MESH)

    for offset in range(1, shards):
        pl.semaphore_signal(
            barrier,
            inc=1,
            device_id={"dp": lax.rem(mine + offset, shards)},
            device_id_type=MESH,
        )

    edge = jnp.zeros((4, images, width, 3 * GW), jnp.bfloat16)
    taps[:, :, 0:width, :] = edge
    taps[:, :, pad - width : pad, :] = edge
    acc[...] = jnp.zeros_like(acc)

    greeted = jnp.where(has_below, 1, 0) + jnp.where(is_top, 0, 1) + (shards - 1)
    pl.semaphore_wait(barrier, greeted)

    column = lax.rem(lax.broadcasted_iota(jnp.int32, (rows, GW), 0), width)
    at_left = column == 0
    at_right = column == width - 1

    def put_taps(slot, wide):
        left = jnp.where(at_left, 0.0, pltpu.roll(wide, 1, 0))
        right = jnp.where(at_right, 0.0, pltpu.roll(wide, rows - 1, 0))
        for place, piece in enumerate((left, wide, right)):
            taps[slot, :, width : width + cells, place * GW : (place + 1) * GW] = piece.astype(
                jnp.bfloat16
            ).reshape(images, cells, GW)

    def slab(slot):
        return jnp.concatenate(
            [
                taps[slot, :, row * width : row * width + cells, :].reshape(rows, 3 * GW)
                for row in range(3)
            ],
            axis=1,
        )

    def conv(slot, branch, group):
        return lax.dot_general(
            slab(slot),
            weights[branch, group],
            (((1,), (0,)), ((), ())),
            preferred_element_type=jnp.float32,
        )

    def conv_t(slot, branch, group):
        view = jnp.concatenate(
            [weights[branch, group, (8 - k) * GW : (9 - k) * GW, :] for k in range(9)], axis=1
        )
        return lax.dot_general(
            slab(slot),
            view,
            (((1,), (1,)), ((), ())),
            preferred_element_type=jnp.float32,
        )

    def add_term(branch, group, slot, grad):
        acc[branch, group] += lax.dot_general(
            grad,
            slab(slot),
            (((0,), (0,)), ((), ())),
            preferred_element_type=jnp.float32,
        )

    @pl.loop(0, ticks * groups)
    def _(step):
        inner = lax.rem(step, WIDTH * ticks)
        tick = inner // WIDTH
        group = (step // (WIDTH * ticks)) * WIDTH + lax.rem(inner, WIDTH)

        @pl.when(tick == 0)
        def _():
            for stream in range(4):
                first_copy(group, stream).wait()
            for branch in range(2):
                weight_copy(group, branch).wait()

        @pl.when(jnp.logical_and(tick > 0, is_top))
        def _():
            for stream in range(4):
                feed_copy(tick, group, stream).wait()

        @pl.when(jnp.logical_and(tick > 0, jnp.logical_not(is_top)))
        def _():
            for stream in range(4):
                below_copy(tick - 1, group, stream).wait_recv()

        def give(stream, value):
            outbuf[tick, group, stream] = value

            @pl.when(jnp.logical_and(tick < ticks - 1, has_below))
            def _():
                below_copy(tick, group, stream).start()

            @pl.when(tick == ticks - 1)
            def _():
                final_copy(group, stream).start()

        one = inbuf[tick, group, 0].astype(jnp.float32)
        grad_two = inbuf[tick, group, 3]
        put_taps(0, jax.nn.silu(one).astype(jnp.bfloat16).astype(jnp.float32))
        put_taps(1, grad_two.astype(jnp.float32))
        two = inbuf[tick, group, 1].astype(jnp.float32)
        input_two = (two - conv(0, 1, group)).astype(jnp.bfloat16)
        give(1, input_two)
        wide_two = input_two.astype(jnp.float32)
        put_taps(2, jax.nn.silu(wide_two).astype(jnp.bfloat16).astype(jnp.float32))
        total_one = (
            inbuf[tick, group, 2].astype(jnp.float32) + conv_t(1, 1, group) * smooth_grad(one)
        ).astype(jnp.bfloat16)
        give(2, total_one)
        put_taps(3, total_one.astype(jnp.float32))
        input_one = (one - conv(2, 0, group)).astype(jnp.bfloat16)
        give(0, input_one)
        total_two = (
            grad_two.astype(jnp.float32) + conv_t(3, 0, group) * smooth_grad(wide_two)
        ).astype(jnp.bfloat16)
        give(3, total_two)
        add_term(0, group, 2, total_one)
        add_term(1, group, 0, grad_two)

        @pl.when(tick == ticks - 1)
        def _():
            for branch in range(2):
                for k in range(9):
                    block = acc[branch, group, :, k * GW : (k + 1) * GW].T * (1.0 / cells)
                    gown[branch, group, k * GW : (k + 1) * GW, :] = block
                    gsend[branch, group, k * GW : (k + 1) * GW, :] = block.astype(jnp.bfloat16)
                for offset in range(1, shards):
                    share_copy(group, branch, offset).start()

    @pl.loop(0, groups)
    def _(group):
        for branch in range(2):
            total = gown[branch, group, pl.ds(pl.multiple_of(mine * share, 16), share), :]
            for offset in range(1, shards):
                share_copy(group, branch, offset).wait_recv()
                total = total + grecv[offset - 1, branch, group].astype(jnp.float32)
            gout[branch, group] = total
            gout_copy(group, branch).start()

    @pl.loop(0, groups)
    def _(group):
        for branch in range(2):
            gout_copy(group, branch).wait()
            for offset in range(1, shards):
                share_copy(group, branch, offset).wait_send()
        for stream in range(4):
            final_copy(group, stream).wait()

        @pl.when(has_below)
        def _():
            for tick in range(ticks - 1):
                for stream in range(4):
                    below_copy(tick, group, stream).wait_send()


def on_device(section_states, conv_kernels, top_feed):
    _, _, images, height, width, chans = section_states.shape
    ticks = top_feed.shape[0] + 1
    groups = chans // GW
    shards = lax.axis_size("dp")
    taps_rows = conv_kernels.shape[2]
    share = taps_rows // shards
    rows = images * height * width
    states = section_states.reshape(4, rows, chans)
    feed = top_feed.reshape(ticks - 1, 4, rows, chans)
    dims = (ticks, groups, images, height, width, share, shards)
    anywhere = pl.BlockSpec(memory_space=pl.ANY)
    dma = pltpu.SemaphoreType.DMA
    final, grads = pl.pallas_call(
        functools.partial(fused_kernel, dims),
        out_shape=(
            jax.ShapeDtypeStruct((4, rows, chans), jnp.bfloat16),
            jax.ShapeDtypeStruct((2, share, chans), jnp.float32),
        ),
        in_specs=[anywhere] * 3,
        out_specs=[anywhere] * 2,
        scratch_shapes=[
            pltpu.VMEM((ticks, groups, 4, rows, GW), jnp.bfloat16),
            pltpu.VMEM((ticks, groups, 4, rows, GW), jnp.bfloat16),
            pltpu.VMEM((2, groups, taps_rows, GW), jnp.bfloat16),
            pltpu.VMEM((4, images, (height + 2) * width, 3 * GW), jnp.bfloat16),
            pltpu.VMEM((2, groups, GW, taps_rows), jnp.float32),
            pltpu.VMEM((2, groups, taps_rows, GW), jnp.bfloat16),
            pltpu.VMEM((2, groups, taps_rows, GW), jnp.float32),
            pltpu.VMEM((max(shards - 1, 1), 2, groups, share, GW), jnp.bfloat16),
            pltpu.VMEM((2, groups, share, GW), jnp.float32),
            dma((ticks, groups, 4)),
            dma((ticks, groups, 4)),
            dma((2, groups)),
            dma((groups, 4)),
            dma((max(shards - 1, 1), 2, groups)),
            dma((max(shards - 1, 1), 2, groups)),
            dma((2, groups)),
        ],
        compiler_params=pltpu.CompilerParams(
            collective_id=0, has_side_effects=True, vmem_limit_bytes=56 * 1024 * 1024
        ),
    )(states, conv_kernels[0], feed)
    return (
        final.reshape(section_states.shape),
        grads.reshape(1, 2, share, chans),
    )


def solution(mesh):
    return jax.shard_map(
        on_device,
        mesh=mesh,
        in_specs=(
            P("section", None, "dp", None, None, None),
            P("section", None, None, None),
            P(None, None, "dp", None, None, None),
        ),
        out_specs=(P("section", None, "dp", None, None, None), P("section", None, "dp", None)),
        check_vma=False,
    )
```

```python
import functools

import jax
import jax.numpy as jnp
from jax import lax
from jax.experimental import pallas as pl
from jax.experimental.pallas import tpu as pltpu
from jax.sharding import PartitionSpec as P

GW = 128
MESH = pl.DeviceIdType.MESH


def smooth_grad(value):
    sigma = jax.nn.sigmoid(value)
    return sigma * (1.0 + value * (1.0 - sigma))


def steps_in_order(groups, ticks):
    tuned = ((0, 0), (1, 0), (2, 0), (0, 1), (1, 1), (0, 2), (2, 1), (1, 2), (0, 3), (3, 0), (2, 2), (1, 3), (3, 1), (2, 3), (3, 2), (3, 3))
    if sorted(tuned) == [(group, tick) for group in range(groups) for tick in range(ticks)]:
        return tuned
    return [(group, tick) for tick in range(ticks) for group in range(groups)]


def fused_kernel(
    dims,
    states_ref,
    kernels_ref,
    feed_ref,
    final_ref,
    grads_ref,
    inbuf,
    outbuf,
    weights,
    flipped,
    taps,
    acc,
    gsend,
    gown,
    grecv,
    in_sem,
    send_sem,
    weight_sem,
    gsend_sem,
    grecv_sem,
):
    ticks, groups, images, height, width, share, shards = dims
    cells = height * width
    order = steps_in_order(groups, ticks)
    rows = images * cells
    pad = (height + 2) * width
    me = lax.axis_index("section")
    count = lax.axis_size("section")
    mine = lax.axis_index("dp")
    is_top = me == count - 1
    has_below = me > 0

    def lanes(group):
        start = group * GW
        return pl.ds(start if isinstance(group, int) else pl.multiple_of(start, GW), GW)

    def first_copy(group, stream):
        return pltpu.make_async_copy(
            states_ref.at[stream, :, lanes(group)],
            inbuf.at[0, group, stream],
            in_sem.at[0, group, stream],
        )

    def feed_copy(tick, group, stream):
        return pltpu.make_async_copy(
            feed_ref.at[tick - 1, stream, :, lanes(group)],
            inbuf.at[tick, group, stream],
            in_sem.at[tick, group, stream],
        )

    def weight_copy(group, branch):
        return pltpu.make_async_copy(
            kernels_ref.at[branch, :, lanes(group)],
            weights.at[branch, group],
            weight_sem.at[branch, group],
        )

    def below_copy(tick, group, stream):
        return pltpu.make_async_remote_copy(
            src_ref=outbuf.at[tick, group, stream],
            dst_ref=inbuf.at[tick + 1, group, stream],
            send_sem=send_sem.at[tick, group, stream],
            recv_sem=in_sem.at[tick + 1, group, stream],
            device_id={"section": me - 1},
            device_id_type=MESH,
        )

    def share_copy(group, branch, offset):
        partner = lax.rem(mine + offset, shards)
        return pltpu.make_async_remote_copy(
            src_ref=gsend.at[branch, group, pl.ds(pl.multiple_of(partner * share, 16), share)],
            dst_ref=grecv.at[offset - 1, branch, group],
            send_sem=gsend_sem.at[offset - 1, branch, group],
            recv_sem=grecv_sem.at[offset - 1, branch, group],
            device_id={"dp": partner},
            device_id_type=MESH,
        )

    for group in range(groups):
        for stream in range(4):
            first_copy(group, stream).start()
        for branch in range(2):
            weight_copy(group, branch).start()

    @pl.when(is_top)
    def _():
        @pl.loop(1, ticks)
        def _(tick):
            for group in range(groups):
                for stream in range(4):
                    feed_copy(tick, group, stream).start()

    barrier = pltpu.get_barrier_semaphore()

    @pl.when(has_below)
    def _():
        pl.semaphore_signal(barrier, inc=1, device_id={"section": me - 1}, device_id_type=MESH)

    @pl.when(jnp.logical_not(is_top))
    def _():
        pl.semaphore_signal(barrier, inc=1, device_id={"section": me + 1}, device_id_type=MESH)

    for offset in range(1, shards):
        pl.semaphore_signal(
            barrier,
            inc=1,
            device_id={"dp": lax.rem(mine + offset, shards)},
            device_id_type=MESH,
        )

    edge = jnp.zeros((4, images, width, 3 * GW), jnp.bfloat16)
    taps[:, :, 0:width, :] = edge
    taps[:, :, pad - width : pad, :] = edge
    acc[...] = jnp.zeros_like(acc)

    greeted = jnp.where(has_below, 1, 0) + jnp.where(is_top, 0, 1) + (shards - 1)
    column = lax.rem(lax.broadcasted_iota(jnp.int32, (rows, GW), 0), width)
    at_left = column == 0
    at_right = column == width - 1

    def put_taps(slot, wide):
        left = jnp.where(at_left, 0.0, pltpu.roll(wide, 1, 0))
        right = jnp.where(at_right, 0.0, pltpu.roll(wide, rows - 1, 0))
        for place, piece in enumerate((left, wide, right)):
            taps[slot, :, width : width + cells, place * GW : (place + 1) * GW] = piece.astype(
                jnp.bfloat16
            ).reshape(images, cells, GW)

    def slab(slot):
        return jnp.concatenate(
            [
                taps[slot, :, row * width : row * width + cells, :].reshape(rows, 3 * GW)
                for row in range(3)
            ],
            axis=1,
        )

    def conv(slot, branch, group):
        return lax.dot_general(
            slab(slot),
            weights[branch, group],
            (((1,), (0,)), ((), ())),
            preferred_element_type=jnp.float32,
        )

    def conv_t(slot, branch, group):
        return lax.dot_general(
            slab(slot),
            flipped[branch, group],
            (((1,), (0,)), ((), ())),
            preferred_element_type=jnp.float32,
        )

    def add_term(branch, group, slot, grad):
        acc[branch, group] += lax.dot_general(
            grad,
            slab(slot),
            (((0,), (0,)), ((), ())),
            preferred_element_type=jnp.float32,
        )

    @pl.loop(0, ticks * groups)
    def _(step):
        tick = jnp.int32(0)
        group = jnp.int32(0)
        for place, (at_group, at_tick) in enumerate(order):
            tick = jnp.where(step == place, at_tick, tick)
            group = jnp.where(step == place, at_group, group)

        @pl.when(tick == 0)
        def _():
            for stream in range(4):
                first_copy(group, stream).wait()
            for branch in range(2):
                weight_copy(group, branch).wait()
                for k in range(9):
                    flipped[branch, group, k * GW : (k + 1) * GW, :] = weights[
                        branch, group, (8 - k) * GW : (9 - k) * GW, :
                    ].T

        @pl.when(jnp.logical_and(tick > 0, is_top))
        def _():
            for stream in range(4):
                feed_copy(tick, group, stream).wait()

        @pl.when(jnp.logical_and(tick > 0, jnp.logical_not(is_top)))
        def _():
            for stream in range(4):
                below_copy(tick - 1, group, stream).wait_recv()

        def give(stream, value):
            outbuf[tick, group, stream] = value

            @pl.when(jnp.logical_and(tick < ticks - 1, has_below))
            def _():
                below_copy(tick, group, stream).start()

            @pl.when(tick == ticks - 1)
            def _():
                final_ref[stream, :, lanes(group)] = value

        def hand_on(branch):
            @pl.when(tick == ticks - 1)
            def _():
                for k in range(9):
                    block = acc[branch, group, :, k * GW : (k + 1) * GW].T * (1.0 / cells)
                    gown[branch, group, k * GW : (k + 1) * GW, :] = block
                    gsend[branch, group, k * GW : (k + 1) * GW, :] = block.astype(jnp.bfloat16)
                for offset in range(1, shards):
                    share_copy(group, branch, offset).start()

        one = inbuf[tick, group, 0].astype(jnp.float32)
        grad_two = inbuf[tick, group, 3]
        put_taps(0, jax.nn.silu(one).astype(jnp.bfloat16).astype(jnp.float32))
        put_taps(1, grad_two.astype(jnp.float32))
        two = inbuf[tick, group, 1].astype(jnp.float32)
        input_two = (two - conv(0, 1, group)).astype(jnp.bfloat16)

        @pl.when(step == 0)
        def _():
            pl.semaphore_wait(barrier, greeted)

        give(1, input_two)
        add_term(1, group, 0, grad_two)
        hand_on(1)
        wide_two = input_two.astype(jnp.float32)
        put_taps(2, jax.nn.silu(wide_two).astype(jnp.bfloat16).astype(jnp.float32))
        total_one = (
            inbuf[tick, group, 2].astype(jnp.float32) + conv_t(1, 1, group) * smooth_grad(one)
        ).astype(jnp.bfloat16)
        give(2, total_one)
        put_taps(3, total_one.astype(jnp.float32))
        input_one = (one - conv(2, 0, group)).astype(jnp.bfloat16)
        give(0, input_one)
        total_two = (
            grad_two.astype(jnp.float32) + conv_t(3, 0, group) * smooth_grad(wide_two)
        ).astype(jnp.bfloat16)
        give(3, total_two)
        add_term(0, group, 2, total_one)
        hand_on(0)

    @pl.loop(0, groups)
    def _(group):
        for branch in (1, 0):
            total = gown[branch, group, pl.ds(pl.multiple_of(mine * share, 16), share), :]
            for offset in range(1, shards):
                share_copy(group, branch, offset).wait_recv()
                total = total + grecv[offset - 1, branch, group].astype(jnp.float32)
            grads_ref[branch, :, lanes(group)] = total

    @pl.loop(0, groups)
    def _(group):
        for branch in range(2):
            for offset in range(1, shards):
                share_copy(group, branch, offset).wait_send()
        @pl.when(has_below)
        def _():
            for tick in range(ticks - 1):
                for stream in range(4):
                    below_copy(tick, group, stream).wait_send()


def on_device(section_states, conv_kernels, top_feed):
    _, _, images, height, width, chans = section_states.shape
    ticks = top_feed.shape[0] + 1
    groups = chans // GW
    shards = lax.axis_size("dp")
    taps_rows = conv_kernels.shape[2]
    share = taps_rows // shards
    rows = images * height * width
    states = section_states.reshape(4, rows, chans)
    feed = top_feed.reshape(ticks - 1, 4, rows, chans)
    dims = (ticks, groups, images, height, width, share, shards)
    anywhere = pl.BlockSpec(memory_space=pltpu.HBM)
    dma = pltpu.SemaphoreType.DMA
    final, grads = pl.pallas_call(
        functools.partial(fused_kernel, dims),
        out_shape=(
            pltpu.VMEM((4, rows, chans), jnp.bfloat16),
            pltpu.VMEM((2, share, chans), jnp.float32),
        ),
        in_specs=[anywhere] * 3,
        out_specs=[pl.BlockSpec(memory_space=pltpu.VMEM)] * 2,
        scratch_shapes=[
            pltpu.VMEM((ticks, groups, 4, rows, GW), jnp.bfloat16),
            pltpu.VMEM((ticks, groups, 4, rows, GW), jnp.bfloat16),
            pltpu.VMEM((2, groups, taps_rows, GW), jnp.bfloat16),
            pltpu.VMEM((2, groups, taps_rows, GW), jnp.bfloat16),
            pltpu.VMEM((4, images, (height + 2) * width, 3 * GW), jnp.bfloat16),
            pltpu.VMEM((2, groups, GW, taps_rows), jnp.float32),
            pltpu.VMEM((2, groups, taps_rows, GW), jnp.bfloat16),
            pltpu.VMEM((2, groups, taps_rows, GW), jnp.float32),
            pltpu.VMEM((max(shards - 1, 1), 2, groups, share, GW), jnp.bfloat16),
            dma((ticks, groups, 4)),
            dma((ticks, groups, 4)),
            dma((2, groups)),
            dma((max(shards - 1, 1), 2, groups)),
            dma((max(shards - 1, 1), 2, groups)),
        ],
        compiler_params=pltpu.CompilerParams(
            collective_id=0, has_side_effects=True, vmem_limit_bytes=56 * 1024 * 1024
        ),
    )(states, conv_kernels[0], feed)
    return (
        final.reshape(section_states.shape),
        grads.reshape(1, 2, share, chans),
    )


def solution(mesh):
    return jax.shard_map(
        on_device,
        mesh=mesh,
        in_specs=(
            P("section", None, "dp", None, None, None),
            P("section", None, None, None),
            P(None, None, "dp", None, None, None),
        ),
        out_specs=(P("section", None, "dp", None, None, None), P("section", None, "dp", None)),
        check_vma=False,
    )
```

```python
import functools

import jax
import jax.numpy as jnp
from jax import lax
from jax.experimental import pallas as pl
from jax.experimental.pallas import tpu as pltpu
from jax.sharding import PartitionSpec as P

GW = 128
MESH = pl.DeviceIdType.MESH


def smooth_grad(value):
    sigma = jax.nn.sigmoid(value)
    return sigma * (1.0 + value * (1.0 - sigma))


def steps_in_order(groups, ticks):
    tuned = ((0, 0), (1, 0), (0, 1), (2, 0), (0, 2), (1, 1), (0, 3), (2, 1), (1, 2), (3, 0), (1, 3), (2, 2), (3, 1), (2, 3), (3, 2), (3, 3))
    if sorted(tuned) == [(group, tick) for group in range(groups) for tick in range(ticks)]:
        return tuned
    return [(group, tick) for tick in range(ticks) for group in range(groups)]


def fused_kernel(
    dims,
    states_ref,
    kernels_ref,
    feed_ref,
    final_ref,
    grads_ref,
    inbuf,
    outbuf,
    weights,
    flipped,
    taps,
    acc,
    gsend,
    gown,
    grecv,
    in_sem,
    send_sem,
    weight_sem,
    gsend_sem,
    grecv_sem,
):
    ticks, groups, images, height, width, share, shards = dims
    cells = height * width
    order = steps_in_order(groups, ticks)
    sends = ((1, 2), (0, 1), (3, 1))
    rows = images * cells
    pad = (height + 2) * width
    me = lax.axis_index("section")
    count = lax.axis_size("section")
    mine = lax.axis_index("dp")
    is_top = me == count - 1
    has_below = me > 0

    def lanes(group):
        start = group * GW
        return pl.ds(start if isinstance(group, int) else pl.multiple_of(start, GW), GW)

    def first_copy(group, stream):
        return pltpu.make_async_copy(
            states_ref.at[stream, :, lanes(group)],
            inbuf.at[0, group, stream],
            in_sem.at[0, group, stream],
        )

    def feed_copy(tick, group, stream):
        return pltpu.make_async_copy(
            feed_ref.at[tick - 1, stream, :, lanes(group)],
            inbuf.at[tick, group, stream],
            in_sem.at[tick, group, stream],
        )

    def weight_copy(group, branch):
        return pltpu.make_async_copy(
            kernels_ref.at[branch, :, lanes(group)],
            weights.at[branch, group],
            weight_sem.at[branch, group],
        )

    def below_copy(tick, group, stream, size):
        return pltpu.make_async_remote_copy(
            src_ref=outbuf.at[tick, group, pl.ds(stream, size)],
            dst_ref=inbuf.at[tick + 1, group, pl.ds(stream, size)],
            send_sem=send_sem.at[tick, group, stream],
            recv_sem=in_sem.at[tick + 1, group, stream],
            device_id={"section": me - 1},
            device_id_type=MESH,
        )

    def share_copy(group, branch, offset):
        partner = lax.rem(mine + offset, shards)
        return pltpu.make_async_remote_copy(
            src_ref=gsend.at[branch, group, pl.ds(pl.multiple_of(partner * share, 16), share)],
            dst_ref=grecv.at[offset - 1, branch, group],
            send_sem=gsend_sem.at[offset - 1, branch, group],
            recv_sem=grecv_sem.at[offset - 1, branch, group],
            device_id={"dp": partner},
            device_id_type=MESH,
        )

    for group in range(groups):
        for stream in range(4):
            first_copy(group, stream).start()
        for branch in range(2):
            weight_copy(group, branch).start()

    @pl.when(is_top)
    def _():
        @pl.loop(1, ticks)
        def _(tick):
            for group in range(groups):
                for stream in range(4):
                    feed_copy(tick, group, stream).start()

    barrier = pltpu.get_barrier_semaphore()

    @pl.when(has_below)
    def _():
        pl.semaphore_signal(barrier, inc=1, device_id={"section": me - 1}, device_id_type=MESH)

    @pl.when(jnp.logical_not(is_top))
    def _():
        pl.semaphore_signal(barrier, inc=1, device_id={"section": me + 1}, device_id_type=MESH)

    for offset in range(1, shards):
        pl.semaphore_signal(
            barrier,
            inc=1,
            device_id={"dp": lax.rem(mine + offset, shards)},
            device_id_type=MESH,
        )

    edge = jnp.zeros((4, images, width, 3 * GW), jnp.bfloat16)
    taps[:, :, 0:width, :] = edge
    taps[:, :, pad - width : pad, :] = edge
    acc[...] = jnp.zeros_like(acc)

    greeted = jnp.where(has_below, 1, 0) + jnp.where(is_top, 0, 1) + (shards - 1)
    column = lax.rem(lax.broadcasted_iota(jnp.int32, (rows, GW), 0), width)
    at_left = column == 0
    at_right = column == width - 1

    def put_taps(slot, wide):
        left = jnp.where(at_left, 0.0, pltpu.roll(wide, 1, 0))
        right = jnp.where(at_right, 0.0, pltpu.roll(wide, rows - 1, 0))
        for place, piece in enumerate((left, wide, right)):
            taps[slot, :, width : width + cells, place * GW : (place + 1) * GW] = piece.astype(
                jnp.bfloat16
            ).reshape(images, cells, GW)

    def slab(slot):
        return jnp.concatenate(
            [
                taps[slot, :, row * width : row * width + cells, :].reshape(rows, 3 * GW)
                for row in range(3)
            ],
            axis=1,
        )

    def conv(slot, branch, group):
        return lax.dot_general(
            slab(slot),
            weights[branch, group],
            (((1,), (0,)), ((), ())),
            preferred_element_type=jnp.float32,
        )

    def conv_t(slot, branch, group):
        return lax.dot_general(
            slab(slot),
            flipped[branch, group],
            (((1,), (0,)), ((), ())),
            preferred_element_type=jnp.float32,
        )

    def add_term(branch, group, slot, grad):
        acc[branch, group] += lax.dot_general(
            grad,
            slab(slot),
            (((0,), (0,)), ((), ())),
            preferred_element_type=jnp.float32,
        )

    @pl.loop(0, ticks * groups)
    def _(step):
        word = jnp.int32(0)
        for place in range(0, len(order), 3):
            packed = 0
            for at, (at_group, at_tick) in enumerate(order[place : place + 3]):
                packed |= (at_group * 32 + at_tick) << (10 * at)
            word = jnp.where(step >= place, packed, word)
        entry = lax.shift_right_logical(word, 10 * lax.rem(step, 3))
        tick = entry & 31
        group = lax.shift_right_logical(entry, 5) & 31

        @pl.when(tick == 0)
        def _():
            for stream in range(4):
                first_copy(group, stream).wait()
            for branch in range(2):
                weight_copy(group, branch).wait()
                for k in range(9):
                    flipped[branch, group, k * GW : (k + 1) * GW, :] = weights[
                        branch, group, (8 - k) * GW : (9 - k) * GW, :
                    ].T

        @pl.when(jnp.logical_and(tick > 0, is_top))
        def _():
            for stream in range(4):
                feed_copy(tick, group, stream).wait()

        @pl.when(jnp.logical_and(tick > 0, jnp.logical_not(is_top)))
        def _():
            for stream, size in sends:
                below_copy(tick - 1, group, stream, size).wait_recv()

        def give(first, size):
            @pl.when(jnp.logical_and(tick < ticks - 1, has_below))
            def _():
                below_copy(tick, group, first, size).start()

            @pl.when(tick == ticks - 1)
            def _():
                for stream in range(first, first + size):
                    final_ref[stream, :, lanes(group)] = outbuf[tick, group, stream]

        def hand_on(branch):
            @pl.when(tick == ticks - 1)
            def _():
                for k in range(9):
                    block = acc[branch, group, :, k * GW : (k + 1) * GW].T * (1.0 / cells)
                    gown[branch, group, k * GW : (k + 1) * GW, :] = block
                    gsend[branch, group, k * GW : (k + 1) * GW, :] = block.astype(jnp.bfloat16)
                for offset in range(1, shards):
                    share_copy(group, branch, offset).start()

        one = inbuf[tick, group, 0].astype(jnp.float32)
        grad_two = inbuf[tick, group, 3]
        put_taps(0, jax.nn.silu(one).astype(jnp.bfloat16).astype(jnp.float32))
        put_taps(1, grad_two.astype(jnp.float32))
        two = inbuf[tick, group, 1].astype(jnp.float32)
        input_two = (two - conv(0, 1, group)).astype(jnp.bfloat16)
        outbuf[tick, group, 1] = input_two
        put_taps(2, jax.nn.silu(input_two.astype(jnp.float32)).astype(jnp.bfloat16).astype(jnp.float32))
        total_one = (
            inbuf[tick, group, 2].astype(jnp.float32) + conv_t(1, 1, group) * smooth_grad(one)
        ).astype(jnp.bfloat16)
        outbuf[tick, group, 2] = total_one
        put_taps(3, total_one.astype(jnp.float32))
        add_term(1, group, 0, inbuf[tick, group, 3])

        @pl.when(step == 0)
        def _():
            pl.semaphore_wait(barrier, greeted)

        give(1, 2)
        hand_on(1)
        outbuf[tick, group, 0] = (
            inbuf[tick, group, 0].astype(jnp.float32) - conv(2, 0, group)
        ).astype(jnp.bfloat16)
        outbuf[tick, group, 3] = (
            inbuf[tick, group, 3].astype(jnp.float32)
            + conv_t(3, 0, group) * smooth_grad(outbuf[tick, group, 1].astype(jnp.float32))
        ).astype(jnp.bfloat16)
        give(0, 1)
        give(3, 1)
        add_term(0, group, 2, outbuf[tick, group, 2])
        hand_on(0)

    @pl.loop(0, groups)
    def _(group):
        for branch in (1, 0):
            total = gown[branch, group, pl.ds(pl.multiple_of(mine * share, 16), share), :]
            for offset in range(1, shards):
                share_copy(group, branch, offset).wait_recv()
                total = total + grecv[offset - 1, branch, group].astype(jnp.float32)
            grads_ref[branch, :, lanes(group)] = total

    @pl.loop(0, groups)
    def _(group):
        for branch in range(2):
            for offset in range(1, shards):
                share_copy(group, branch, offset).wait_send()
        @pl.when(has_below)
        def _():
            for tick in range(ticks - 1):
                for stream, size in sends:
                    below_copy(tick, group, stream, size).wait_send()


def on_device(section_states, conv_kernels, top_feed):
    _, _, images, height, width, chans = section_states.shape
    ticks = top_feed.shape[0] + 1
    groups = chans // GW
    shards = lax.axis_size("dp")
    taps_rows = conv_kernels.shape[2]
    share = taps_rows // shards
    rows = images * height * width
    states = section_states.reshape(4, rows, chans)
    feed = top_feed.reshape(ticks - 1, 4, rows, chans)
    dims = (ticks, groups, images, height, width, share, shards)
    anywhere = pl.BlockSpec(memory_space=pltpu.HBM)
    dma = pltpu.SemaphoreType.DMA
    final, grads = pl.pallas_call(
        functools.partial(fused_kernel, dims),
        out_shape=(
            pltpu.VMEM((4, rows, chans), jnp.bfloat16),
            pltpu.VMEM((2, share, chans), jnp.float32),
        ),
        in_specs=[anywhere] * 3,
        out_specs=[pl.BlockSpec(memory_space=pltpu.VMEM)] * 2,
        scratch_shapes=[
            pltpu.VMEM((ticks, groups, 4, rows, GW), jnp.bfloat16),
            pltpu.VMEM((ticks, groups, 4, rows, GW), jnp.bfloat16),
            pltpu.VMEM((2, groups, taps_rows, GW), jnp.bfloat16),
            pltpu.VMEM((2, groups, taps_rows, GW), jnp.bfloat16),
            pltpu.VMEM((4, images, (height + 2) * width, 3 * GW), jnp.bfloat16),
            pltpu.VMEM((2, groups, GW, taps_rows), jnp.float32),
            pltpu.VMEM((2, groups, taps_rows, GW), jnp.bfloat16),
            pltpu.VMEM((2, groups, taps_rows, GW), jnp.float32),
            pltpu.VMEM((max(shards - 1, 1), 2, groups, share, GW), jnp.bfloat16),
            dma((ticks, groups, 4)),
            dma((ticks, groups, 4)),
            dma((2, groups)),
            dma((max(shards - 1, 1), 2, groups)),
            dma((max(shards - 1, 1), 2, groups)),
        ],
        compiler_params=pltpu.CompilerParams(
            collective_id=0, has_side_effects=True, vmem_limit_bytes=56 * 1024 * 1024
        ),
    )(states, conv_kernels[0], feed)
    return (
        final.reshape(section_states.shape),
        grads.reshape(1, 2, share, chans),
    )


def solution(mesh):
    return jax.shard_map(
        on_device,
        mesh=mesh,
        in_specs=(
            P("section", None, "dp", None, None, None),
            P("section", None, None, None),
            P(None, None, "dp", None, None, None),
        ),
        out_specs=(P("section", None, "dp", None, None, None), P("section", None, "dp", None)),
        check_vma=False,
    )
```
